32 devices in a mesh: grp: 4 (over z), mem: 8 (over y, x, core).
Axes of the slice: x: 2, y: 2, z: 4, core: 2. Of those that a mesh axis runs over, the one named last changes fastest.
Arguments:
- embeddings: bfloat16 [32768, 4096], P(('grp', 'mem')), may hold values from -6 to 6
- local_picks: int32 [4, 64], P('grp', 'mem'), may hold values from 0 to 1023
- second_picks: int32 [4, 16], P('grp'), may hold values from 0 to 63
- final_picks: int32 [16], replicated, may hold values from 0 to 63
Outputs:
- gain_table: float32 [64, 64], P('grp', 'mem')
- final_cover: float32 [32768], P(('grp', 'mem'))
The draws below stay inside these ranges and needn't reach their ends.
Inputs may be any that keep to these rules, and one draw needn't show every extreme that they name: `local_picks`: entry (g, m * 8 + k) names a row among the 1024 points of device m of group g; repeats may occur. `second_picks`: candidate indices of the group, in greedy order; repeats may occur. `final_picks`: index g * 16 + t names group g's second-round pick t; repeats may occur.
All inputs are finite; a program needn't handle non-finite values.
Results may differ from the reference program's by a relative error of at most 0.0003.
Values may be sent and summed in bfloat16 or wider, within the bound.
No kernel may reach another device: no remote copies, remote signals or barrier semaphores. Data moves between devices by JAX's collectives and lax.ppermute only.
A program may use at most 64 MiB of HBM per device.

```python
import jax
import jax.numpy as jnp
from jax import lax

D = 4096
P_DEV = 1024
K1 = 8
K2 = 16
K3 = 16
CANDS = 64
UNION = 64
POINTS = 32768
N_GRP = 4
N_MEM = 8


def plant(result, own_key, low, top_value):
    spot = [jax.random.randint(jax.random.fold_in(own_key, axis), (), 0, length) for axis, length in enumerate(result.shape)]
    widest = result.shape.index(max(result.shape))
    beside = spot[:widest] + [(spot[widest] + 1) % result.shape[widest]] + spot[widest + 1:]
    return result.at[tuple(spot)].set(low).at[tuple(beside)].set(top_value)


def steps_of(key, shape, pieces, low, largest):
    level, own = 1.0, jax.random.fold_in(key, 6)
    for position, blocks in pieces:
        heights = jnp.exp(jax.random.uniform(jax.random.fold_in(own, position), (blocks,), jnp.float32, low / len(pieces), largest / len(pieces)))
        level = level * jnp.repeat(heights, shape[position] // blocks).reshape([-1 if axis == position else 1 for axis in range(len(shape))])
    return level


def normal_values(stream_key, shape, spread, most, cuts=(), held_as=jnp.bfloat16):
    drawn = spread * jax.random.normal(stream_key, shape, jnp.float32)
    if cuts:
        drawn = drawn * steps_of(stream_key, shape, cuts, -0.22, 0.18)
    return jnp.clip(drawn, -most, most).astype(held_as)


def setup_inputs(seed: int = 0) -> dict:
    key_list = jax.random.split(jax.random.key(seed), 5)
    embeddings = normal_values(key_list[0], (POINTS, D), 1.0, 6.0, ((0, 32),))
    local_picks = plant(jax.random.randint(key_list[1], (N_GRP, CANDS), 0, P_DEV), jax.random.fold_in(key_list[1], 1), 0, P_DEV - 1).astype(jnp.int32)
    second_picks = plant(jax.random.randint(key_list[2], (N_GRP, K2), 0, CANDS), jax.random.fold_in(key_list[2], 1), 0, CANDS - 1).astype(jnp.int32)
    final_picks = plant(jax.random.randint(key_list[3], (K3,), 0, UNION), jax.random.fold_in(key_list[3], 1), 0, UNION - 1).astype(jnp.int32)
    return {"embeddings": embeddings, "local_picks": local_picks, "second_picks": second_picks, "final_picks": final_picks}


def reference(embeddings, local_picks, second_picks, final_picks):
    scaling = float(D) ** -0.5
    grouped = embeddings.reshape(N_GRP, N_MEM, P_DEV, D)
    pick_rows = local_picks.reshape(N_GRP, N_MEM, K1).astype(jnp.int32)
    candidates = jax.vmap(jax.vmap(lambda points, chosen: jnp.take(points, chosen, axis=0)))(grouped, pick_rows)
    candidates = candidates.reshape(N_GRP, CANDS, D)
    winners = jax.vmap(lambda cands, chosen: jnp.take(cands, chosen, axis=0))(candidates, second_picks.astype(jnp.int32))
    winners = winners.reshape(UNION, D)
    final_rows = jnp.take(winners, final_picks.astype(jnp.int32), axis=0)

    def group_gains(inputs):
        cand_group, points_group, second_group = inputs

        def device_step(running, device_inputs):
            point_rows, member = device_inputs
            similar_map = jnp.dot(point_rows, cand_group.T, preferred_element_type=jnp.float32) * scaling
            own_block = lax.dynamic_slice_in_dim(similar_map, member * K1, K1, 1)
            coverage = jnp.max(own_block, axis=1)
            chosen_cols = jnp.take(similar_map, second_group, axis=1)

            def greedy_step(cover_now, column):
                partial_value = jnp.sum(jnp.maximum(similar_map - cover_now[:, None], 0.0), axis=0)
                return jnp.maximum(cover_now, column), partial_value

            _, partials = lax.scan(greedy_step, coverage, chosen_cols.T)
            return running + partials, None

        start_sum = jnp.zeros((K2, CANDS), jnp.float32)
        running, _ = lax.scan(device_step, start_sum, (points_group, jnp.arange(N_MEM, dtype=jnp.int32)))
        return running / P_DEV

    gain_table = lax.map(group_gains, (candidates, grouped, second_picks.astype(jnp.int32)))
    gain_table = gain_table.reshape(N_GRP * K2, CANDS)

    def device_cover(point_rows):
        return jnp.max(jnp.dot(point_rows, final_rows.T, preferred_element_type=jnp.float32) * scaling, axis=1)

    final_cover = lax.map(device_cover, embeddings.reshape(N_GRP * N_MEM, P_DEV, D)).reshape(POINTS)
    return gain_table, final_cover
```

```python
import jax
import jax.numpy as jnp
from jax import lax
from jax.experimental import pallas as pl
from jax.experimental.pallas import tpu as pltpu
from jax.sharding import PartitionSpec as P


BLOCK = 8
LANES = 128
NT = (((1,), (1,)), ((), ()))
VM = pl.BlockSpec(memory_space=pltpu.VMEM)
SM = pl.BlockSpec(memory_space=pltpu.SMEM)
PARAMS = pltpu.CompilerParams(vmem_limit_bytes=16 * 1024 * 1024)


def pick_kernel(picks_ref, emb_ref, out_ref, buf, sems):
    count = out_ref.shape[0]

    def copy(k):
        start = pl.multiple_of((picks_ref[0, k] // BLOCK) * BLOCK, BLOCK)
        return pltpu.make_async_copy(emb_ref.at[pl.ds(start, BLOCK), :], buf.at[k], sems.at[k])

    for k in range(count):
        copy(k).start()
    sub = lax.broadcasted_iota(jnp.int32, (count, 1), 0)
    rows = jnp.zeros(out_ref.shape, jnp.float32)
    for k in range(count):
        copy(k).wait()
        shift = (k - picks_ref[0, k]) % BLOCK
        rows = jnp.where(sub == k, pltpu.roll(buf[k].astype(jnp.float32), shift, 0), rows)
    out_ref[...] = rows.astype(out_ref.dtype)


def pick_rows(embeddings, local_picks):
    count, width = local_picks.shape[1], embeddings.shape[1]
    return pl.pallas_call(
        pick_kernel,
        compiler_params=pltpu.CompilerParams(vmem_limit_bytes=60 * 1024 * 1024),
        out_shape=jax.ShapeDtypeStruct((count, width), embeddings.dtype),
        in_specs=[SM, pl.BlockSpec(memory_space=pl.ANY)],
        out_specs=VM,
        scratch_shapes=[
            pltpu.VMEM((count, BLOCK, width), embeddings.dtype),
            pltpu.SemaphoreType.DMA((count,)),
        ],
    )(local_picks, embeddings)


def column(pick, member, own, n_mem):
    rel = lax.div(pick, own) ^ member
    return ((rel >> 1) + (rel & 1) * (n_mem // 2)) * own + lax.rem(pick, own)


def table_kernel(own, n_mem, ids_ref, second_ref, final_ref, emb_ref, out_ref):
    steps, count = second_ref.shape[1], final_ref.shape[0]
    spot = lax.broadcasted_iota(jnp.int32, out_ref.shape, 0)
    lane = lax.broadcasted_iota(jnp.int32, out_ref.shape, 1)
    want = jnp.full(out_ref.shape, -1, jnp.int32)
    for k in range(count):
        at = final_ref[k]
        col = column(second_ref[0, lax.rem(at, steps)], ids_ref[0], own, n_mem)
        want = jnp.where(spot == k, jnp.where(lax.div(at, steps) == ids_ref[1], col, -1), want)
    out_ref[...] = (want == lane).astype(jnp.float32).astype(out_ref.dtype)


def pick_table(ids, second, final_picks, embeddings, own, n_mem):
    return pl.pallas_call(
        lambda *refs: table_kernel(own, n_mem, *refs),
        compiler_params=PARAMS,
        out_shape=jax.ShapeDtypeStruct((final_picks.shape[0], n_mem * own), embeddings.dtype),
        in_specs=[SM, SM, SM, VM],
        out_specs=VM,
    )(ids, second, final_picks, embeddings)


def gain_kernel(n_blocks, scaling, ids_ref, second_ref, emb_ref, *refs):
    blocks, outs, sim_ref = refs[:n_blocks], refs[n_blocks:-1], refs[-1]
    own = blocks[0].shape[0]
    cands, points = sim_ref.shape
    steps = second_ref.shape[1]
    rows = jnp.concatenate([b[...] for b in blocks], 0)
    sim_ref[...] = lax.dot_general(rows, emb_ref[...], NT, preferred_element_type=jnp.float32) * scaling
    cover = jnp.max(sim_ref[0:own, :], axis=0, keepdims=True)
    lane = lax.broadcasted_iota(jnp.int32, (cands, steps), 1)
    result = jnp.zeros((cands, steps), jnp.float32)
    for t in range(steps):
        total = jnp.zeros((cands, LANES), jnp.float32)
        for at in range(0, points, LANES):
            part = slice(at, at + LANES)
            total = total + jnp.maximum(sim_ref[:, part] - cover[:, part], 0.0)
        summed = jnp.sum(total, axis=1, keepdims=True)
        result = jnp.where(lane == t, summed, result)
        col = column(second_ref[0, t], ids_ref[0], own, n_blocks)
        cover = jnp.maximum(cover, sim_ref[pl.ds(col, 1), :])
    each = cands // len(outs)
    for i, out in enumerate(outs):
        out[...] = result[i * each : (i + 1) * each]


def gains(ids, second, embeddings, blocks, scaling):
    n, own = len(blocks), blocks[0].shape[0]
    points, width = embeddings.shape
    steps = second.shape[1]
    body = lambda *refs: gain_kernel(n, scaling, *refs)
    return pl.pallas_call(
        body,
        compiler_params=PARAMS,
        out_shape=[jax.ShapeDtypeStruct((n * own // 2, steps), jnp.float32)] * 2,
        in_specs=[SM, SM] + [VM] * (n + 1),
        out_specs=[VM, VM],
        scratch_shapes=[pltpu.VMEM((n * own, points), jnp.float32)],
        cost_estimate=pl.CostEstimate(
            flops=8 * 2 * n * own * points * width, transcendentals=0, bytes_accessed=2 * embeddings.size
        ),
    )(ids, second, embeddings, *blocks)


def final_kernel(scaling, ids_ref, mine_ref, other_ref, emb_ref, out_ref, rows_ref):
    half = mine_ref.shape[1]
    core = ids_ref[0] & 1
    rows_ref[:, pl.ds(pl.multiple_of(core * half, LANES), half)] = mine_ref[...]
    rows_ref[:, pl.ds(pl.multiple_of((1 - core) * half, LANES), half)] = other_ref[...]
    sim = lax.dot_general(rows_ref[...], emb_ref[...], NT, preferred_element_type=jnp.float32)
    out_ref[...] = jnp.max(sim * scaling, axis=0)


def final(ids, mine, other, embeddings, scaling):
    count, _ = mine.shape
    points, width = embeddings.shape
    body = lambda *refs: final_kernel(scaling, *refs)
    return pl.pallas_call(
        body,
        compiler_params=PARAMS,
        out_shape=jax.ShapeDtypeStruct((points,), jnp.float32),
        in_specs=[SM] + [VM] * 3,
        out_specs=VM,
        scratch_shapes=[pltpu.VMEM((count, width), mine.dtype)],
        cost_estimate=pl.CostEstimate(
            flops=8 * 2 * 64 * points * width, transcendentals=0, bytes_accessed=2 * embeddings.size
        ),
    )(ids, mine, other, embeddings)


def build(n_grp, n_mem):
    def swap(x, axis, size, mask):
        return lax.ppermute(x, axis, [(i, i ^ mask) for i in range(size)])

    masks = [1 << b for b in range(1, n_mem.bit_length() - 1)]
    rounds = []
    for at in range(0, len(masks), 2):
        pair = masks[at : at + 2]
        rounds.append(pair + ([pair[0] ^ pair[1]] if len(pair) == 2 else []))

    def per_device(embeddings, local_picks, second_picks, final_picks):
        points, width = embeddings.shape
        scaling = float(width) ** -0.5
        own = local_picks.shape[1]
        half_count = n_mem // 2
        order = [2 * i for i in range(half_count)] + [2 * i + 1 for i in range(half_count)]
        member = lax.axis_index("mem").astype(jnp.int32)
        ids = jnp.stack([member, lax.axis_index("grp").astype(jnp.int32)])
        side = (member & 1) * (width // 2)
        picks, ids, side = lax.optimization_barrier((local_picks, ids, side))

        blocks = {0: pick_rows(embeddings, picks)}
        table = pick_table(ids, second_picks, final_picks, embeddings, own, n_mem)
        emb = embeddings
        for reach in rounds:
            held = sorted(blocks)
            for mask in reach:
                for j in held:
                    blocks[j ^ mask] = swap(blocks[j], "mem", n_mem, mask)
        for j in sorted(blocks):
            blocks[j ^ 1] = swap(blocks[j], "mem", n_mem, 1)
        ordered = [blocks[j] for j in order]

        part = lax.dynamic_slice_in_dim(
            jnp.concatenate(ordered, 0), side, width // 2, 1
        )
        final_half = jnp.dot(table, part, preferred_element_type=jnp.float32).astype(emb.dtype)
        others = [swap(final_half, "grp", n_grp, g) for g in range(1, n_grp)]
        final_half = sum(others, final_half)

        keep, send = gains(ids, second_picks, emb, ordered, scaling)
        final_other = swap(final_half, "mem", n_mem, 1)
        total = keep + swap(send, "mem", n_mem, 1)
        sums = {2 * i: total[i * own : (i + 1) * own] for i in range(half_count)}
        for reach in reversed(rounds):
            gone = 0
            for mask in reach:
                gone |= mask
            stay = {j: [v] for j, v in sums.items() if not j & gone}
            for mask in reach:
                for j in stay:
                    stay[j].append(swap(sums[j ^ mask], "mem", n_mem, mask))
            sums = {j: sum(v[1:], v[0]) for j, v in stay.items()}
        gain_table = sums[0].T / points
        final_cover = final(ids, final_half, final_other, emb, scaling)
        return gain_table, final_cover

    return per_device


def solution(mesh):
    placed = (P(("grp", "mem"), None), P("grp", "mem"), P("grp", None), P())
    body = build(mesh.shape["grp"], mesh.shape["mem"])

    return jax.shard_map(
        body,
        mesh=mesh,
        in_specs=placed,
        out_specs=(P("grp", "mem"), P(("grp", "mem"))),
        check_vma=False,
    )
```
